32 devices in a mesh: row: 8 (over y, x, core), col: 4 (over z).
Axes of the slice: x: 2, y: 2, z: 4, core: 2. Of those that a mesh axis runs over, the one named last changes fastest.
Arguments:
- integrals: float32 [1024, 8, 8192], P(None, 'row', 'col'), may hold values from -6 to 6, as said below
- amplitudes: float32 [1024, 8, 8192], P(None, 'row', 'col'), as said below
- tile_lists: int32 [4, 3], replicated, may hold values from 0 to 3, as said below
- gap_index: int32 [8192], replicated, may hold values from 0 to 511
- pair_gaps: float32 [512], replicated, may hold values from 0.5 to 4
Outputs:
- updated: float32 [1024, 8, 8192], P(None, 'row', 'col')
The draws below stay inside these ranges and needn't reach their ends.
Inputs may be any that keep to these rules, and one draw needn't show every extreme that they name: `integrals`: symmetric matrix. `amplitudes`: symmetric matrix. `tile_lists`: row t holds 3 distinct tile indices, among them t itself; s appears in row t exactly when t appears in row s.
All inputs are finite; a program needn't handle non-finite values.
Results may differ from the reference program's by a relative error of at most 0.0036.
Values may be sent and summed in bfloat16 or wider, within the bound.
A program may use at most 192 MiB of HBM per device.

```python
import math
import jax
import jax.numpy as jnp
from jax import lax

N = 8192
NE = 512
TILE = 2048
NT = 4
K = 3
RCYC = 1024


def symmetric_field(key):
    first_key = jax.random.fold_in(key, 0)
    base = jax.random.normal(first_key, (N, N), jnp.float32)
    field = (base + base.T) * 0.7071
    return jnp.clip(field, -6.0, 6.0)


def draw_integrals(key, part):
    field = symmetric_field(jax.random.fold_in(key, 11))
    return field.reshape(RCYC, N // RCYC, N)


def draw_amplitudes(key, part):
    field = symmetric_field(jax.random.fold_in(key, 23)) * (1.5 / jnp.sqrt(jnp.float32(N)))
    return field.reshape(RCYC, N // RCYC, N)


def draw_tile_lists(key, part):
    order = jax.random.permutation(jax.random.fold_in(key, 37), NT).astype(jnp.int32)
    place = jnp.argsort(order).astype(jnp.int32)
    offsets = jnp.arange(K, dtype=jnp.int32) - (K - 1) // 2
    return order[(place[:, None] + offsets[None, :]) % NT].astype(jnp.int32)


def set_ends(result, rng, low, largest):
    spot = [jax.random.randint(jax.random.fold_in(rng, axis), (), 0, length) for axis, length in enumerate(result.shape)]
    widest = result.shape.index(max(result.shape))
    next_to = spot[:widest] + [(spot[widest] + 1) % result.shape[widest]] + spot[widest + 1:]
    return result.at[tuple(spot)].set(low).at[tuple(next_to)].set(largest)


def setup_inputs(seed: int = 0) -> dict:
    seeds = jax.random.split(jax.random.key(seed), 6)
    return {
        "integrals": draw_integrals(jax.random.fold_in(seeds[5], 71), 0),
        "amplitudes": draw_amplitudes(jax.random.fold_in(seeds[5], 71), 0),
        "tile_lists": draw_tile_lists(jax.random.fold_in(seeds[5], 71), 0),
        "gap_index": set_ends(jax.random.randint(seeds[3], (N,), 0, NE), jax.random.fold_in(seeds[3], 1), 0, NE - 1).astype(jnp.int32),
        "pair_gaps": jnp.clip(jnp.exp(jax.random.uniform(seeds[4], (NE,), jnp.float32, math.log(0.5), math.log(4.0))), 0.5, 4.0),
    }


def reference(integrals, amplitudes, tile_lists, gap_index, pair_gaps):
    matrix_order = integrals.shape[0] * integrals.shape[1]
    full_int = integrals.reshape(matrix_order, matrix_order)
    full_amp = amplitudes.reshape(matrix_order, matrix_order)
    tile_range = jnp.arange(NT, dtype=jnp.int32)
    screen_cols = jnp.max((tile_lists[:, :, None] == tile_range[None, None, :]).astype(jnp.float32), axis=1)
    tile_ids = jnp.arange(matrix_order, dtype=jnp.int32) // TILE
    by_col = screen_cols[tile_ids]
    cell_mask = by_col[:, tile_ids].T
    int_low = lax.optimization_barrier(full_int.astype(jnp.bfloat16)).astype(jnp.float32)
    amp_low = lax.optimization_barrier((full_amp * cell_mask).astype(jnp.bfloat16)).astype(jnp.float32)
    coupled = jnp.dot(int_low, amp_low, precision=lax.Precision.HIGHEST)
    residual = full_int + coupled + coupled.T
    gap_values = pair_gaps[gap_index]
    updated = -residual / (gap_values[:, None] + gap_values[None, :])
    return updated.reshape(integrals.shape)
```

```python
import functools

import jax
import jax.numpy as jnp
from jax import lax
from jax.experimental import pallas as pl
from jax.experimental.pallas import tpu as pltpu
from jax.sharding import PartitionSpec as P


VMEM_LIMIT = 60 * 1024 * 1024


def lookup_gaps(indices, pair_gaps):
    table_ids = jnp.arange(pair_gaps.shape[0], dtype=jnp.int32)
    return jnp.sum(
        jnp.where(indices[:, None] == table_ids[None, :], pair_gaps[None, :], 0.0), axis=1
    )


def deal(order, stride, transposed):
    q = lax.broadcasted_iota(jnp.int32, (order, order), 1 if transposed else 0)
    m = lax.broadcasted_iota(jnp.int32, (order, order), 0 if transposed else 1)
    return (m == (q % stride) * (order // stride) + q // stride).astype(jnp.bfloat16)


def contract_kernel(
    stride, terms, has_init, last, tile_tbl, slot_tbl, pos_tbl, valid_tbl, *refs
):
    mats, refs = refs[: 1 + last], refs[1 + last :]
    v_ref, refs = refs[0], refs[1:]
    if has_init:
        init_ref, refs = refs[0], refs[1:]
    if last:
        out_ref, send_ref, perm_ref = refs
    else:
        (out_ref,) = refs
    n, s, j = pl.program_id(0), pl.program_id(1), pl.program_id(2)
    entry = s * terms + j
    if last:

        @pl.when((n == 0) & (s == 0) & (j == 0))
        def _():
            perm_ref[...] = deal(perm_ref.shape[0], stride, False)

    @pl.when(j == 0)
    def _():
        out_ref[...] = init_ref[...] if has_init else jnp.zeros_like(out_ref)

    @pl.when(valid_tbl[entry] == 1)
    def _():
        left = mats[0][...] if not last else mats[0][...] + mats[1][...]
        block = v_ref[:, tile_tbl[entry]]
        block = block.reshape(block.shape[0] * block.shape[1], block.shape[2])
        out_ref[...] += jnp.dot(left, block, preferred_element_type=jnp.float32)

    if last:

        @pl.when(j == terms - 1)
        def _():
            dealt = jnp.dot(
                out_ref[...].astype(jnp.bfloat16),
                perm_ref[...],
                preferred_element_type=jnp.float32,
            ).astype(jnp.bfloat16)
            width = send_ref.shape[2]
            for r in range(stride):
                send_ref[r] = dealt[:, r * width : (r + 1) * width]


def contract(mats, gathered, tables, init, last):
    stride, tiles, per_tile, width = gathered.shape
    terms = tables[0].shape[0] // tiles
    nb = min(width, 128 * stride)
    mat_spec = pl.BlockSpec(
        (None, None, per_tile, width),
        lambda n, s, j, kt, st, pt, vt: (st[s * terms + j], pt[s * terms + j], 0, 0),
    )
    out_spec = pl.BlockSpec((per_tile, nb), lambda n, s, j, *_: (s, n))
    in_specs = [mat_spec] * len(mats) + [
        pl.BlockSpec((stride, tiles, per_tile, nb), lambda n, s, j, *_: (0, 0, 0, n))
    ]
    args = list(mats) + [gathered]
    if init is not None:
        in_specs.append(out_spec)
        args.append(init)
    out_shape = [jax.ShapeDtypeStruct((tiles * per_tile, width), jnp.float32)]
    out_specs = [out_spec]
    scratch = []
    if last:
        out_shape.append(
            jax.ShapeDtypeStruct((stride, tiles * per_tile, width // stride), jnp.bfloat16)
        )
        out_specs.append(
            pl.BlockSpec((stride, per_tile, nb // stride), lambda n, s, j, *_: (0, s, n))
        )
        scratch.append(pltpu.VMEM((nb, nb), jnp.bfloat16))
    flops = 2 * per_tile * width * width * (tiles if last else tiles * terms)
    return pl.pallas_call(
        functools.partial(contract_kernel, stride, terms, init is not None, last),
        out_shape=out_shape,
        grid_spec=pltpu.PrefetchScalarGridSpec(
            num_scalar_prefetch=4,
            grid=(width // nb, tiles, terms),
            in_specs=in_specs,
            out_specs=out_specs,
            scratch_shapes=scratch,
        ),
        compiler_params=pltpu.CompilerParams(
            dimension_semantics=("arbitrary",) * 3, vmem_limit_bytes=VMEM_LIMIT
        ),
        cost_estimate=pl.CostEstimate(
            flops=flops, bytes_accessed=2 * gathered.size, transcendentals=0
        ),
    )(*tables, *args)


def finish_kernel(stride, x_ref, v_ref, c_ref, gr_ref, gc_ref, out_ref, perm_ref):
    @pl.when((pl.program_id(0) == 0) & (pl.program_id(1) == 0))
    def _():
        perm_ref[...] = deal(perm_ref.shape[0], stride, True)

    x = x_ref[...].reshape(perm_ref.shape[0], x_ref.shape[2])
    mirrored = lax.dot_general(
        x, perm_ref[...], (((0,), (0,)), ((), ())), preferred_element_type=jnp.float32
    )
    residual = v_ref[...] + c_ref[...] + mirrored
    out_ref[...] = -residual / (gr_ref[...] + gc_ref[...])


def finish(arrived, values, product, gap_rows, gap_cols):
    tiles, stride, per_tile, _ = arrived.shape
    rows, width = values.shape
    nb = min(width, 128 * stride)
    tile_spec = pl.BlockSpec((per_tile, nb), lambda c, n: (c, n))
    return pl.pallas_call(
        functools.partial(finish_kernel, stride),
        out_shape=jax.ShapeDtypeStruct((rows, width), jnp.float32),
        grid=(tiles, width // nb),
        in_specs=[
            pl.BlockSpec((None, stride, nb // stride, per_tile), lambda c, n: (c, 0, n, 0)),
            tile_spec,
            tile_spec,
            pl.BlockSpec((per_tile, 1), lambda c, n: (c, 0)),
            pl.BlockSpec((1, nb), lambda c, n: (0, n)),
        ],
        out_specs=tile_spec,
        scratch_shapes=[pltpu.VMEM((nb, nb), jnp.bfloat16)],
        compiler_params=pltpu.CompilerParams(
            dimension_semantics=("arbitrary",) * 2, vmem_limit_bytes=VMEM_LIMIT
        ),
    )(arrived, values, product, gap_rows[:, None], gap_cols[None, :])


def per_device(integrals, amplitudes, tile_lists, gap_index, pair_gaps):
    rows, _, width = integrals.shape
    stride = lax.axis_size("row")
    tiles = lax.axis_size("col")
    row_place = lax.axis_index("row")
    col_place = lax.axis_index("col")
    terms = tile_lists.shape[1]
    per_tile = width // stride

    values = integrals[:, 0, :]
    gathered = lax.all_gather(values.astype(jnp.bfloat16), "row", axis=0, tiled=False)
    gathered = gathered.reshape(stride, tiles, per_tile, width)

    my_list = lax.dynamic_slice_in_dim(tile_lists, col_place, 1, 0)[0]
    amp_tiles = amplitudes[:, 0, :].astype(jnp.bfloat16).reshape(tiles, per_tile, width)
    compact = amp_tiles[my_list].reshape(terms * per_tile, width)
    own = (
        jnp.dot(compact, deal(width, stride, False), preferred_element_type=jnp.float32)
        .astype(jnp.bfloat16)
        .reshape(terms, per_tile, width)
    )

    from_left, from_right = own, own
    slots = [own]
    for step in range(1, tiles):
        up = [(i, i + 1) for i in range(step - 1, tiles - 1)]
        down = [(tiles - 1 - a, tiles - 1 - b) for a, b in up]
        from_left = lax.ppermute(from_left, "col", up)
        from_right = lax.ppermute(from_right, "col", down)
        if step < tiles - 1:
            slots += [from_left, from_right]

    tile_tbl = tile_lists.reshape(-1)
    row_tile = jnp.repeat(jnp.arange(tiles, dtype=jnp.int32), terms)
    pos_tbl = jnp.argmax(tile_lists[tile_tbl] == row_tile[:, None], axis=1).astype(jnp.int32)
    offset = col_place - tile_tbl
    far = jnp.abs(offset) == tiles - 1
    slot_tbl = jnp.where(offset > 0, 2 * offset - 1, -2 * offset)
    near_valid = (~far).astype(jnp.int32)
    far_valid = far.astype(jnp.int32)
    near = (tile_tbl, jnp.where(far, 0, slot_tbl), pos_tbl, near_valid)
    distant = (tile_tbl, jnp.zeros_like(slot_tbl), pos_tbl * far_valid, far_valid)

    (partial,) = contract([jnp.stack(slots)], gathered, near, None, False)
    product, dealt = contract(
        [from_left[None], from_right[None]], gathered, distant, partial, True
    )

    arrived = lax.all_to_all(dealt, "row", split_axis=0, concat_axis=0, tiled=True)
    arrived = arrived.reshape(stride, tiles, per_tile, per_tile)
    arrived = lax.all_to_all(arrived, "col", split_axis=1, concat_axis=0, tiled=True)
    arrived = arrived.reshape(tiles, stride, per_tile, per_tile)

    index_rows = lax.dynamic_slice_in_dim(gap_index.reshape(rows, stride), row_place, 1, 1)[:, 0]
    index_cols = lax.dynamic_slice_in_dim(gap_index, col_place * width, width, 0)
    gap_rows = lookup_gaps(index_rows, pair_gaps)
    gap_cols = lookup_gaps(index_cols, pair_gaps)
    return finish(arrived, values, product, gap_rows, gap_cols)[:, None, :]


def solution(mesh):
    placed = (P(None, "row", "col"), P(None, "row", "col"), P(), P(), P())
    return jax.shard_map(
        per_device, mesh=mesh, in_specs=placed, out_specs=P(None, "row", "col"), check_vma=False
    )
```

```python
import functools

import jax
import jax.numpy as jnp
from jax import lax
from jax.experimental import pallas as pl
from jax.experimental.pallas import tpu as pltpu
from jax.sharding import PartitionSpec as P


VMEM_LIMIT = 60 * 1024 * 1024


def lookup_gaps(indices, pair_gaps):
    table_ids = jnp.arange(pair_gaps.shape[0], dtype=jnp.int32)
    return jnp.sum(
        jnp.where(indices[:, None] == table_ids[None, :], pair_gaps[None, :], 0.0), axis=1
    )


def deal(order, stride, transposed):
    q = lax.broadcasted_iota(jnp.int32, (order, order), 1 if transposed else 0)
    m = lax.broadcasted_iota(jnp.int32, (order, order), 0 if transposed else 1)
    return (m == (q % stride) * (order // stride) + q // stride).astype(jnp.bfloat16)


def contract_kernel(
    stride, terms, has_init, last, tile_tbl, slot_tbl, pos_tbl, valid_tbl, *refs
):
    mats, refs = refs[: 1 + last], refs[1 + last :]
    v_ref, refs = refs[0], refs[1:]
    if has_init:
        init_ref, refs = refs[0], refs[1:]
    if last:
        out_ref, send_ref, perm_ref = refs
    else:
        (out_ref,) = refs
    n, s, j = pl.program_id(0), pl.program_id(1), pl.program_id(2)
    entry = s * terms + j
    if last:

        @pl.when((n == 0) & (s == 0) & (j == 0))
        def _():
            perm_ref[...] = deal(perm_ref.shape[0], stride, False)

    @pl.when(j == 0)
    def _():
        out_ref[...] = init_ref[...] if has_init else jnp.zeros_like(out_ref)

    @pl.when(valid_tbl[entry] == 1)
    def _():
        left = mats[0][...] if not last else mats[0][...] + mats[1][...]
        block = v_ref[...] if last else v_ref[:, tile_tbl[entry]]
        block = block.reshape(block.shape[0] * block.shape[1], block.shape[2])
        out_ref[...] += jnp.dot(left, block, preferred_element_type=jnp.float32)

    if last:

        @pl.when(j == terms - 1)
        def _():
            dealt = jnp.dot(
                out_ref[...].astype(jnp.bfloat16),
                perm_ref[...],
                preferred_element_type=jnp.float32,
            ).astype(jnp.bfloat16)
            width = send_ref.shape[2]
            for r in range(stride):
                send_ref[r] = dealt[:, r * width : (r + 1) * width]


def contract(mats, gathered, tables, init, last):
    stride, tiles, per_tile, width = gathered.shape
    terms = tables[0].shape[0] // tiles
    nb = min(width, 128 * stride)
    mat_spec = pl.BlockSpec(
        (None, None, per_tile, width),
        lambda n, s, j, kt, st, pt, vt: (st[s * terms + j], pt[s * terms + j], 0, 0),
    )
    out_spec = pl.BlockSpec((per_tile, nb), lambda n, s, j, *_: (s, n))
    if last:
        v_spec = pl.BlockSpec(
            (stride, None, per_tile, nb), lambda n, s, j, kt, *_: (0, kt[0], 0, n)
        )
    else:
        v_spec = pl.BlockSpec((stride, tiles, per_tile, nb), lambda n, s, j, *_: (0, 0, 0, n))
    in_specs = [mat_spec] * len(mats) + [v_spec]
    args = list(mats) + [gathered]
    if init is not None:
        in_specs.append(out_spec)
        args.append(init)
    out_shape = [jax.ShapeDtypeStruct((tiles * per_tile, width), jnp.float32)]
    out_specs = [out_spec]
    scratch = []
    if last:
        out_shape.append(
            jax.ShapeDtypeStruct((stride, tiles * per_tile, width // stride), jnp.bfloat16)
        )
        out_specs.append(
            pl.BlockSpec((stride, per_tile, nb // stride), lambda n, s, j, *_: (0, s, n))
        )
        scratch.append(pltpu.VMEM((nb, nb), jnp.bfloat16))
    flops = 2 * per_tile * width * width * (tiles if last else tiles * terms)
    return pl.pallas_call(
        functools.partial(contract_kernel, stride, terms, init is not None, last),
        out_shape=out_shape,
        grid_spec=pltpu.PrefetchScalarGridSpec(
            num_scalar_prefetch=4,
            grid=(width // nb, tiles, terms),
            in_specs=in_specs,
            out_specs=out_specs,
            scratch_shapes=scratch,
        ),
        compiler_params=pltpu.CompilerParams(
            dimension_semantics=("arbitrary",) * 3, vmem_limit_bytes=VMEM_LIMIT
        ),
        cost_estimate=pl.CostEstimate(
            flops=flops, bytes_accessed=2 * gathered.size, transcendentals=0
        ),
    )(*tables, *args)


def select_kernel(stride, list_ref, a_ref, out_ref, perm_ref):
    @pl.when(pl.program_id(0) == 0)
    def _():
        perm_ref[...] = deal(perm_ref.shape[0], stride, False)

    nb = perm_ref.shape[0]
    width = a_ref.shape[1]
    part = nb // stride
    for n in range(width // nb):
        dealt = jnp.dot(
            a_ref[:, n * nb : (n + 1) * nb].astype(jnp.bfloat16),
            perm_ref[...],
            preferred_element_type=jnp.float32,
        ).astype(jnp.bfloat16)
        for r in range(stride):
            base = r * (width // stride) + n * part
            out_ref[:, base : base + part] = dealt[:, r * part : (r + 1) * part]


def select(amps, my_list, stride, tiles):
    rows, width = amps.shape
    per_tile = rows // tiles
    terms = my_list.shape[0]
    nb = min(width, 128 * stride)
    return pl.pallas_call(
        functools.partial(select_kernel, stride),
        out_shape=jax.ShapeDtypeStruct((terms, per_tile, width), jnp.bfloat16),
        grid_spec=pltpu.PrefetchScalarGridSpec(
            num_scalar_prefetch=1,
            grid=(terms,),
            in_specs=[pl.BlockSpec((per_tile, width), lambda j, ml: (ml[j], 0))],
            out_specs=pl.BlockSpec((None, per_tile, width), lambda j, ml: (j, 0, 0)),
            scratch_shapes=[pltpu.VMEM((nb, nb), jnp.bfloat16)],
        ),
        compiler_params=pltpu.CompilerParams(
            dimension_semantics=("arbitrary",), vmem_limit_bytes=VMEM_LIMIT
        ),
    )(my_list, amps)


def exchange_kernel(rows_axis, cols_axis, src, dst, send_sem, recv_sem, own_sem):
    per_tile = dst.shape[2]
    count = rows_axis * cols_axis
    row, col = lax.axis_index("row"), lax.axis_index("col")
    me = row * cols_axis + col

    def place(offset):
        peer = lax.rem(me + offset, count)
        return peer // cols_axis, lax.rem(peer, cols_axis)

    barrier = pltpu.get_barrier_semaphore()

    def greet(offset, carry):
        r, c = place(offset)
        pl.semaphore_signal(barrier, inc=1, device_id={"row": r, "col": c})
        return carry

    lax.fori_loop(1, count, greet, 0)
    pl.semaphore_wait(barrier, count - 1)

    def block(r, c):
        return src.at[r, pl.ds(pl.multiple_of(c * per_tile, per_tile), per_tile)]

    def remote(offset):
        r, c = place(offset)
        return pltpu.make_async_remote_copy(
            src_ref=block(r, c),
            dst_ref=dst.at[col, row],
            send_sem=send_sem.at[offset],
            recv_sem=recv_sem.at[offset],
            device_id={"row": r, "col": c},
        )

    def begin(offset, carry):
        remote(offset).start()
        return carry

    def end(offset, carry):
        remote(offset).wait()
        return carry

    lax.fori_loop(1, count, begin, 0)
    kept = pltpu.make_async_copy(block(row, col), dst.at[col, row], own_sem)
    kept.start()
    lax.fori_loop(1, count, end, 0)
    kept.wait()


def exchange(dealt, tiles):
    stride, rows, part = dealt.shape
    count = stride * tiles
    return pl.pallas_call(
        functools.partial(exchange_kernel, stride, tiles),
        out_shape=jax.ShapeDtypeStruct((tiles, stride, rows // tiles, part), jnp.bfloat16),
        in_specs=[pl.BlockSpec(memory_space=pl.ANY)],
        out_specs=pl.BlockSpec(memory_space=pl.ANY),
        scratch_shapes=[
            pltpu.SemaphoreType.DMA((count,)),
            pltpu.SemaphoreType.DMA((count,)),
            pltpu.SemaphoreType.DMA,
        ],
        compiler_params=pltpu.CompilerParams(collective_id=0, has_side_effects=True),
    )(dealt)


def finish_kernel(stride, x_ref, v_ref, c_ref, gr_ref, gc_ref, out_ref, perm_ref):
    @pl.when((pl.program_id(0) == 0) & (pl.program_id(1) == 0))
    def _():
        perm_ref[...] = deal(perm_ref.shape[0], stride, True)

    x = x_ref[...].reshape(perm_ref.shape[0], x_ref.shape[2])
    mirrored = lax.dot_general(
        x, perm_ref[...], (((0,), (0,)), ((), ())), preferred_element_type=jnp.float32
    )
    residual = v_ref[...] + c_ref[...] + mirrored
    out_ref[...] = -residual / (gr_ref[...] + gc_ref[...])


def finish(arrived, values, product, gap_rows, gap_cols):
    tiles, stride, per_tile, _ = arrived.shape
    rows, width = values.shape
    nb = min(width, 128 * stride)
    tile_spec = pl.BlockSpec((per_tile, nb), lambda c, n: (c, n))
    return pl.pallas_call(
        functools.partial(finish_kernel, stride),
        out_shape=jax.ShapeDtypeStruct((rows, width), jnp.float32),
        grid=(tiles, width // nb),
        in_specs=[
            pl.BlockSpec((None, stride, nb // stride, per_tile), lambda c, n: (c, 0, n, 0)),
            tile_spec,
            tile_spec,
            pl.BlockSpec((per_tile, 1), lambda c, n: (c, 0)),
            pl.BlockSpec((1, nb), lambda c, n: (0, n)),
        ],
        out_specs=tile_spec,
        scratch_shapes=[pltpu.VMEM((nb, nb), jnp.bfloat16)],
        compiler_params=pltpu.CompilerParams(
            dimension_semantics=("arbitrary",) * 2, vmem_limit_bytes=VMEM_LIMIT
        ),
    )(arrived, values, product, gap_rows[:, None], gap_cols[None, :])


def per_device(integrals, amplitudes, tile_lists, gap_index, pair_gaps):
    rows, _, width = integrals.shape
    stride = lax.axis_size("row")
    tiles = lax.axis_size("col")
    row_place = lax.axis_index("row")
    col_place = lax.axis_index("col")
    terms = tile_lists.shape[1]
    per_tile = width // stride

    values = integrals[:, 0, :]
    gathered = lax.all_gather(values.astype(jnp.bfloat16), "row", axis=0, tiled=False)
    gathered = gathered.reshape(stride, tiles, per_tile, width)

    my_list = lax.dynamic_slice_in_dim(tile_lists, col_place, 1, 0)[0]
    own = select(amplitudes[:, 0, :], my_list, stride, tiles)

    from_left, from_right = own, own
    slots = [own]
    for step in range(1, tiles):
        up = [(i, i + 1) for i in range(step - 1, tiles - 1)]
        down = [(tiles - 1 - a, tiles - 1 - b) for a, b in up]
        from_left = lax.ppermute(from_left, "col", up)
        from_right = lax.ppermute(from_right, "col", down)
        if step < tiles - 1:
            slots += [from_left, from_right]

    tile_tbl = tile_lists.reshape(-1)
    row_tile = jnp.repeat(jnp.arange(tiles, dtype=jnp.int32), terms)
    pos_tbl = jnp.argmax(tile_lists[tile_tbl] == row_tile[:, None], axis=1).astype(jnp.int32)
    offset = col_place - tile_tbl
    far = jnp.abs(offset) == tiles - 1
    slot_tbl = jnp.where(offset > 0, 2 * offset - 1, -2 * offset)
    near_valid = (~far).astype(jnp.int32)
    far_valid = far.astype(jnp.int32)
    near = (tile_tbl, jnp.where(far, 0, slot_tbl), pos_tbl, near_valid)
    far_tile = jnp.where(col_place == 0, tiles - 1, 0)
    distant = (jnp.full_like(tile_tbl, far_tile), jnp.zeros_like(slot_tbl), pos_tbl * far_valid, far_valid)

    index_rows = lax.dynamic_slice_in_dim(gap_index.reshape(rows, stride), row_place, 1, 1)[:, 0]
    index_cols = lax.dynamic_slice_in_dim(gap_index, col_place * width, width, 0)
    gap_rows = lookup_gaps(index_rows, pair_gaps)
    gap_cols = lookup_gaps(index_cols, pair_gaps)
    stacked, values, gap_rows, gap_cols = lax.optimization_barrier(
        (jnp.stack(slots), values, gap_rows, gap_cols)
    )
    (partial,) = contract([stacked], gathered, near, None, False)
    product, dealt = contract(
        [from_left[None], from_right[None]], gathered, distant, partial, True
    )

    arrived = exchange(dealt, tiles)
    return finish(arrived, values, product, gap_rows, gap_cols)[:, None, :]


def solution(mesh):
    placed = (P(None, "row", "col"), P(None, "row", "col"), P(), P(), P())
    return jax.shard_map(
        per_device, mesh=mesh, in_specs=placed, out_specs=P(None, "row", "col"), check_vma=False
    )
```

```python
import functools

import jax
import jax.numpy as jnp
from jax import lax
from jax.experimental import pallas as pl
from jax.experimental.pallas import tpu as pltpu
from jax.sharding import PartitionSpec as P


VMEM_LIMIT = 60 * 1024 * 1024


def lookup_gaps(indices, pair_gaps):
    table_ids = jnp.arange(pair_gaps.shape[0], dtype=jnp.int32)
    return jnp.sum(
        jnp.where(indices[:, None] == table_ids[None, :], pair_gaps[None, :], 0.0), axis=1
    )


def deal(order, stride, transposed):
    q = lax.broadcasted_iota(jnp.int32, (order, order), 1 if transposed else 0)
    m = lax.broadcasted_iota(jnp.int32, (order, order), 0 if transposed else 1)
    return (m == (q % stride) * (order // stride) + q // stride).astype(jnp.bfloat16)


def contract_kernel(
    stride, terms, has_init, last, tile_tbl, slot_tbl, pos_tbl, valid_tbl, *refs
):
    mats, refs = refs[: 1 + last], refs[1 + last :]
    v_ref, refs = refs[0], refs[1:]
    if has_init:
        init_ref, refs = refs[0], refs[1:]
    if last:
        out_ref, send_ref, perm_ref = refs
    else:
        (out_ref,) = refs
    n, s, j = pl.program_id(0), pl.program_id(1), pl.program_id(2)
    entry = s * terms + j
    if last:

        @pl.when((n == 0) & (s == 0) & (j == 0))
        def _():
            perm_ref[...] = deal(perm_ref.shape[0], stride, False)

    @pl.when(j == 0)
    def _():
        out_ref[...] = init_ref[...] if has_init else jnp.zeros_like(out_ref)

    @pl.when(valid_tbl[entry] == 1)
    def _():
        left = mats[0][...] if not last else mats[0][...] + mats[1][...]
        block = v_ref[...] if last else v_ref[:, tile_tbl[entry]]
        block = block.reshape(block.shape[0] * block.shape[1], block.shape[2])
        out_ref[...] += jnp.dot(left, block, preferred_element_type=jnp.float32)

    if last:

        @pl.when(j == terms - 1)
        def _():
            dealt = jnp.dot(
                out_ref[...].astype(jnp.bfloat16),
                perm_ref[...],
                preferred_element_type=jnp.float32,
            ).astype(jnp.bfloat16)
            width = send_ref.shape[2]
            for r in range(stride):
                send_ref[r] = dealt[:, r * width : (r + 1) * width]


def contract(mats, gathered, tables, init, last):
    stride, tiles, per_tile, width = gathered.shape
    terms = tables[0].shape[0] // tiles
    nb = min(width, 128 * stride)
    mat_spec = pl.BlockSpec(
        (None, None, per_tile, width),
        lambda n, s, j, kt, st, pt, vt: (st[s * terms + j], pt[s * terms + j], 0, 0),
    )
    out_spec = pl.BlockSpec((per_tile, nb), lambda n, s, j, *_: (s, n))
    if last:
        v_spec = pl.BlockSpec(
            (stride, None, per_tile, nb), lambda n, s, j, kt, *_: (0, kt[0], 0, n)
        )
    else:
        v_spec = pl.BlockSpec((stride, tiles, per_tile, nb), lambda n, s, j, *_: (0, 0, 0, n))
    in_specs = [mat_spec] * len(mats) + [v_spec]
    args = list(mats) + [gathered]
    if init is not None:
        in_specs.append(out_spec)
        args.append(init)
    out_shape = [jax.ShapeDtypeStruct((tiles * per_tile, width), jnp.float32)]
    out_specs = [out_spec]
    scratch = []
    if last:
        out_shape.append(
            jax.ShapeDtypeStruct((stride, tiles * per_tile, width // stride), jnp.bfloat16)
        )
        out_specs.append(
            pl.BlockSpec((stride, per_tile, nb // stride), lambda n, s, j, *_: (0, s, n))
        )
        scratch.append(pltpu.VMEM((nb, nb), jnp.bfloat16))
    flops = 2 * per_tile * width * width * (tiles if last else tiles * terms)
    return pl.pallas_call(
        functools.partial(contract_kernel, stride, terms, init is not None, last),
        out_shape=out_shape,
        grid_spec=pltpu.PrefetchScalarGridSpec(
            num_scalar_prefetch=4,
            grid=(width // nb, tiles, terms),
            in_specs=in_specs,
            out_specs=out_specs,
            scratch_shapes=scratch,
        ),
        compiler_params=pltpu.CompilerParams(
            dimension_semantics=("arbitrary",) * 3, vmem_limit_bytes=VMEM_LIMIT
        ),
        cost_estimate=pl.CostEstimate(
            flops=flops, bytes_accessed=2 * gathered.size, transcendentals=0
        ),
    )(*tables, *args)


def select_kernel(stride, list_ref, a_ref, out_ref, perm_ref):
    @pl.when(pl.program_id(0) == 0)
    def _():
        perm_ref[...] = deal(perm_ref.shape[0], stride, False)

    nb = perm_ref.shape[0]
    width = a_ref.shape[1]
    part = nb // stride
    for n in range(width // nb):
        dealt = jnp.dot(
            a_ref[:, n * nb : (n + 1) * nb],
            perm_ref[...],
            preferred_element_type=jnp.float32,
        ).astype(jnp.bfloat16)
        for r in range(stride):
            base = r * (width // stride) + n * part
            out_ref[:, base : base + part] = dealt[:, r * part : (r + 1) * part]


def select(amps, my_list, stride, tiles):
    rows, width = amps.shape
    per_tile = rows // tiles
    terms = my_list.shape[0]
    nb = min(width, 128 * stride)
    return pl.pallas_call(
        functools.partial(select_kernel, stride),
        out_shape=jax.ShapeDtypeStruct((terms, per_tile, width), jnp.bfloat16),
        grid_spec=pltpu.PrefetchScalarGridSpec(
            num_scalar_prefetch=1,
            grid=(terms,),
            in_specs=[pl.BlockSpec((per_tile, width), lambda j, ml: (ml[j], 0))],
            out_specs=pl.BlockSpec((None, per_tile, width), lambda j, ml: (j, 0, 0)),
            scratch_shapes=[pltpu.VMEM((nb, nb), jnp.bfloat16)],
        ),
        compiler_params=pltpu.CompilerParams(
            dimension_semantics=("arbitrary",), vmem_limit_bytes=VMEM_LIMIT
        ),
    )(my_list, amps)


def exchange_kernel(
    rows_axis,
    cols_axis,
    src,
    v_hbm,
    c_hbm,
    gr_ref,
    gc_ref,
    out_hbm,
    dst,
    v_buf,
    c_buf,
    out_buf,
    perm_ref,
    send_sem,
    recv_sem,
    own_sem,
    load_sem,
    store_sem,
):
    per_tile = dst.shape[2]
    count = rows_axis * cols_axis
    row, col = lax.axis_index("row"), lax.axis_index("col")
    me = row * cols_axis + col

    def place(offset):
        peer = lax.rem(me + offset, count)
        return peer // cols_axis, lax.rem(peer, cols_axis)

    barrier = pltpu.get_barrier_semaphore()

    def greet(offset, carry):
        r, c = place(offset)
        pl.semaphore_signal(barrier, inc=1, device_id={"row": r, "col": c})
        return carry

    lax.fori_loop(1, count, greet, 0)
    pl.semaphore_wait(barrier, count - 1)

    def tile_rows(c):
        return pl.ds(pl.multiple_of(c * per_tile, per_tile), per_tile)

    def block(r, c):
        return src.at[r, tile_rows(c)]

    def remote(offset):
        r, c = place(offset)
        return pltpu.make_async_remote_copy(
            src_ref=block(r, c),
            dst_ref=dst.at[col, row],
            send_sem=send_sem.at[offset],
            recv_sem=recv_sem.at[offset],
            device_id={"row": r, "col": c},
        )

    def begin(offset, carry):
        remote(offset).start()
        return carry

    lax.fori_loop(1, count, begin, 0)
    kept = pltpu.make_async_copy(block(row, col), dst.at[col, row], own_sem)
    kept.start()
    load_v = pltpu.make_async_copy(v_hbm, v_buf, load_sem.at[0])
    load_c = pltpu.make_async_copy(c_hbm, c_buf, load_sem.at[1])
    load_v.start()
    load_c.start()
    perm_ref[...] = deal(perm_ref.shape[0], rows_axis, True)
    load_v.wait()
    load_c.wait()
    kept.wait()

    nb = perm_ref.shape[0]
    width = v_buf.shape[1]
    part = nb // rows_axis

    def store(c):
        return pltpu.make_async_copy(
            out_buf.at[tile_rows(c)], out_hbm.at[tile_rows(c)], store_sem.at[c]
        )

    def tile(step, carry):
        c = lax.rem(col + step, cols_axis)

        def arrive(r, inner):
            offset = lax.rem(me - (r * cols_axis + c) + count, count)

            @pl.when(offset != 0)
            def _():
                remote(offset).wait_recv()

            return inner

        lax.fori_loop(0, rows_axis, arrive, 0)
        for n in range(width // nb):
            cols = slice(n * nb, (n + 1) * nb)
            x = dst[c, :, n * part : (n + 1) * part, :].reshape(nb, per_tile)
            mirrored = lax.dot_general(
                x, perm_ref[...], (((0,), (0,)), ((), ())), preferred_element_type=jnp.float32
            )
            residual = v_buf[tile_rows(c), cols] + c_buf[tile_rows(c), cols] + mirrored
            out_buf[tile_rows(c), cols] = -residual / (gr_ref[tile_rows(c), :] + gc_ref[:, cols])
        store(c).start()
        return carry

    lax.fori_loop(0, cols_axis, tile, 0)

    def sent(offset, carry):
        remote(offset).wait_send()
        return carry

    def stored(c, carry):
        store(c).wait()
        return carry

    lax.fori_loop(1, count, sent, 0)
    lax.fori_loop(0, cols_axis, stored, 0)


def exchange(dealt, values, product, gap_rows, gap_cols, tiles):
    stride, rows, part = dealt.shape
    width = values.shape[1]
    count = stride * tiles
    nb = min(width, 128 * stride)
    hbm = pl.BlockSpec(memory_space=pl.ANY)
    vmem = pl.BlockSpec(memory_space=pltpu.VMEM)
    return pl.pallas_call(
        functools.partial(exchange_kernel, stride, tiles),
        out_shape=jax.ShapeDtypeStruct((rows, width), jnp.float32),
        in_specs=[hbm, hbm, hbm, vmem, vmem],
        out_specs=hbm,
        scratch_shapes=[
            pltpu.VMEM((tiles, stride, rows // tiles, part), jnp.bfloat16),
            pltpu.VMEM((rows, width), jnp.float32),
            pltpu.VMEM((rows, width), jnp.float32),
            pltpu.VMEM((rows, width), jnp.float32),
            pltpu.VMEM((nb, nb), jnp.bfloat16),
            pltpu.SemaphoreType.DMA((count,)),
            pltpu.SemaphoreType.DMA((count,)),
            pltpu.SemaphoreType.DMA,
            pltpu.SemaphoreType.DMA((2,)),
            pltpu.SemaphoreType.DMA((tiles,)),
        ],
        compiler_params=pltpu.CompilerParams(
            collective_id=0, has_side_effects=True, vmem_limit_bytes=VMEM_LIMIT
        ),
    )(dealt, values, product, gap_rows[:, None], gap_cols[None, :])


def per_device(integrals, amplitudes, tile_lists, gap_index, pair_gaps):
    rows, _, width = integrals.shape
    stride = lax.axis_size("row")
    tiles = lax.axis_size("col")
    row_place = lax.axis_index("row")
    col_place = lax.axis_index("col")
    terms = tile_lists.shape[1]
    per_tile = width // stride

    amps = amplitudes[:, 0, :].astype(jnp.bfloat16)
    amps, integrals = lax.optimization_barrier((amps, integrals))
    values = integrals[:, 0, :]
    gathered = lax.all_gather(values.astype(jnp.bfloat16), "row", axis=0, tiled=False)
    gathered = gathered.reshape(stride, tiles, per_tile, width)

    my_list = lax.dynamic_slice_in_dim(tile_lists, col_place, 1, 0)[0]
    own = select(amps, my_list, stride, tiles)

    from_left, from_right = own, own
    slots = [own]
    for step in range(1, tiles):
        up = [(i, i + 1) for i in range(step - 1, tiles - 1)]
        down = [(tiles - 1 - a, tiles - 1 - b) for a, b in up]
        from_left = lax.ppermute(from_left, "col", up)
        from_right = lax.ppermute(from_right, "col", down)
        if step < tiles - 1:
            slots += [from_left, from_right]

    tile_tbl = tile_lists.reshape(-1)
    row_tile = jnp.repeat(jnp.arange(tiles, dtype=jnp.int32), terms)
    pos_tbl = jnp.argmax(tile_lists[tile_tbl] == row_tile[:, None], axis=1).astype(jnp.int32)
    offset = col_place - tile_tbl
    far = jnp.abs(offset) == tiles - 1
    slot_tbl = jnp.where(offset > 0, 2 * offset - 1, -2 * offset)
    near_valid = (~far).astype(jnp.int32)
    near = (tile_tbl, jnp.where(far, 0, slot_tbl), pos_tbl, near_valid)
    far_tile = jnp.where(col_place == 0, tiles - 1, 0)
    at_end = (col_place == 0) | (col_place == tiles - 1)
    far_list = lax.dynamic_slice_in_dim(tile_lists, far_tile, 1, 0)
    far_hit = far_list == jnp.arange(tiles, dtype=jnp.int32)[:, None]
    distant = (
        jnp.full((tiles,), far_tile, jnp.int32),
        jnp.zeros((tiles,), jnp.int32),
        jnp.argmax(far_hit, axis=1).astype(jnp.int32),
        (jnp.any(far_hit, axis=1) & at_end).astype(jnp.int32),
    )

    index_rows = lax.dynamic_slice_in_dim(gap_index.reshape(rows, stride), row_place, 1, 1)[:, 0]
    index_cols = lax.dynamic_slice_in_dim(gap_index, col_place * width, width, 0)
    gap_rows = lookup_gaps(index_rows, pair_gaps)
    gap_cols = lookup_gaps(index_cols, pair_gaps)
    stacked, values, gap_rows, gap_cols = lax.optimization_barrier(
        (jnp.stack(slots), values, gap_rows, gap_cols)
    )
    (partial,) = contract([stacked], gathered, near, None, False)
    product, dealt = contract(
        [from_left[None], from_right[None]], gathered, distant, partial, True
    )

    return exchange(dealt, values, product, gap_rows, gap_cols, tiles)[:, None, :]


def solution(mesh):
    placed = (P(None, "row", "col"), P(None, "row", "col"), P(), P(), P())
    return jax.shard_map(
        per_device, mesh=mesh, in_specs=placed, out_specs=P(None, "row", "col"), check_vma=False
    )
```
